256 devices in a mesh: seq: 32 (over x, z), head: 8 (over y, core).
Axes of the slice: x: 4, y: 4, z: 8, core: 2. Of those that a mesh axis runs over, the one named last changes fastest.
Arguments:
- hidden_in: bfloat16 [8192, 2048], P('seq'), may hold values from -6 to 6
- w_qk: bfloat16 [2048, 2, 2048], P(None, None, 'head'), may hold values from -0.125 to 0.125
- w_value: bfloat16 [2048, 4096], P(None, 'head'), may hold values from -0.125 to 0.125
- w_outgate: bfloat16 [2048, 4096], P(None, 'head'), may hold values from -0.125 to 0.125
- w_ba: bfloat16 [2048, 2, 32], P(None, None, 'head'), may hold values from -0.125 to 0.125
- conv_qk: bfloat16 [4, 2, 2048], P(None, None, 'head'), may hold values from -3 to 3
- conv_value: bfloat16 [4, 4096], P(None, 'head'), may hold values from -3 to 3
- hist_qk: bfloat16 [3, 2, 2048], P(None, None, 'head'), may hold values from -6 to 6
- hist_value: bfloat16 [3, 4096], P(None, 'head'), may hold values from -6 to 6
- a_log: float32 [32], P('head'), may hold values from -11 to -3
- dt_bias: float32 [32], P('head'), may hold values from -1 to 1
- beta_bias: float32 [32], P('head'), may hold values from -1 to 1
- state_in: float32 [32, 128, 128], P('head'), may hold values from -0.6 to 0.6
- norm_gain: float32 [128], replicated, may hold values from 0.5 to 1.5
- w_out: bfloat16 [4096, 2048], P('head'), may hold values from -0.09375 to 0.09375
Outputs:
- mixed: bfloat16 [8192, 2048], P('seq', 'head')
- checkpoints: float32 [32, 32, 128, 128], P('seq', 'head')
The draws below stay inside these ranges and needn't reach their ends.
All inputs are finite; a program needn't handle non-finite values.
Results may differ from the reference program's by a relative error of at most 0.015.
Values may be sent and summed in bfloat16 or wider, within the bound.
A program may use at most 64 MiB of HBM per device.

```python
import jax
import jax.numpy as jnp
from jax import lax

D = 2048
HK = 16
HV = 32
KEY_HEAD_SIZE = 128
DV = 128
KC = 4
TOK_DEV = 256
KEYW = 2048
VALW = 4096
TOKENS = 8192
N_SEQ = 32
N_HEAD = 8


def block_levels(stream_key, shape, pieces, low, high):
    def one(dim, shards_of):
        heights = jax.random.uniform(jax.random.fold_in(jax.random.fold_in(stream_key, 6), dim), (shards_of,), jnp.float32, low / len(pieces), high / len(pieces))
        return jnp.repeat(jnp.exp(heights), shape[dim] // shards_of).reshape((-1,) + (1,) * (len(shape) - dim - 1))

    level = one(*pieces[0])
    for cut in pieces[1:]:
        level = level * one(*cut)
    return level


def centred(own_key, extent, spread, reach, split=(), dtype=jnp.bfloat16):
    level = block_levels(own_key, extent, split, -0.22, 0.18) if split else 1.0
    values = jax.random.normal(own_key, extent, jnp.float32) * spread * level
    return jnp.minimum(jnp.maximum(values, -reach), reach).astype(dtype)


def setup_inputs(seed: int = 0) -> dict:
    key_of = jax.random.split(jax.random.key(seed), 16)
    return {
        "hidden_in": centred(key_of[0], (TOKENS, D), 1.0, 6.0, ((0, 32),)),
        "w_qk": centred(key_of[1], (D, 2, KEYW), D ** -0.5, 0.125, ((2, 8),)),
        "w_value": centred(key_of[2], (D, VALW), D ** -0.5, 0.125, ((1, 8),)),
        "w_outgate": centred(key_of[3], (D, VALW), D ** -0.5, 0.125, ((1, 8),)),
        "w_ba": centred(key_of[4], (D, 2, HV), D ** -0.5, 0.125, ((2, 8),)),
        "conv_qk": centred(key_of[5], (KC, 2, KEYW), 0.5, 3.0, ((2, 8),)),
        "conv_value": centred(key_of[6], (KC, VALW), 0.5, 3.0, ((1, 8),)),
        "hist_qk": centred(key_of[7], (KC - 1, 2, KEYW), 1.0, 6.0, ((2, 8),)),
        "hist_value": centred(key_of[8], (KC - 1, VALW), 1.0, 6.0, ((1, 8),)),
        "a_log": jnp.clip(-11.0 + 8.0 * jax.random.uniform(key_of[9], (HV,), jnp.float32) ** block_levels(key_of[9], (HV,), ((0, 8),), -0.2, 0.2), -11.0, -3.0),
        "dt_bias": jnp.clip(jax.random.uniform(key_of[10], (HV,), jnp.float32, -1.0, 1.0) * block_levels(key_of[10], (HV,), ((0, 8),), -0.4, 0.0), -1.0, 1.0),
        "beta_bias": jnp.clip(jax.random.uniform(key_of[11], (HV,), jnp.float32, -1.0, 1.0) * block_levels(key_of[11], (HV,), ((0, 8),), -0.4, 0.0), -1.0, 1.0),
        "state_in": centred(key_of[12], (HV, KEY_HEAD_SIZE, DV), 0.1, 0.6, ((0, 8),), jnp.float32),
        "norm_gain": jnp.clip(1.0 + 0.1 * jax.random.normal(key_of[13], (DV,), jnp.float32), 0.5, 1.5),
        "w_out": centred(key_of[14], (VALW, D), VALW ** -0.5, 0.09375, ((0, 8),)),
    }


exact_setting = lax.Precision.HIGHEST

def stored(values):
    return lax.optimization_barrier(values.astype(jnp.bfloat16))

def unit_rows(values):
    return values * lax.rsqrt(lax.optimization_barrier(jnp.sum(values * values, axis=-1, keepdims=True)) + 1e-06)

def causal_filter(history, present, weight):
    joined = jnp.concatenate([history, present], 0).astype(jnp.float32)
    count = present.shape[0]
    total = jnp.zeros(present.shape, jnp.float32)
    for offset in range(weight.shape[0]):
        total = total + weight[offset].astype(jnp.float32) * joined[offset:offset + count]
    return jax.nn.silu(total)

def reference(hidden_in, w_qk, w_value, w_outgate, w_ba, conv_qk, conv_value, hist_qk, hist_value, a_log, dt_bias, beta_bias, state_in, norm_gain, w_out):
    total_rows = hidden_in.shape[0]
    pre_qk = stored(jnp.dot(hidden_in, w_qk.reshape(D, 2 * KEYW), preferred_element_type=jnp.float32))
    pre_value = stored(jnp.dot(hidden_in, w_value, preferred_element_type=jnp.float32))
    mixed_qk = causal_filter(hist_qk.reshape(KC - 1, 2 * KEYW), pre_qk, conv_qk.reshape(KC, 2 * KEYW)).reshape(total_rows, 2, HK, KEY_HEAD_SIZE)
    values = causal_filter(hist_value, pre_value, conv_value).reshape(total_rows, HV, DV)
    queries = jnp.repeat(unit_rows(mixed_qk[:, 0]) * KEY_HEAD_SIZE ** (-0.5), HV // HK, axis=1)
    keys = jnp.repeat(unit_rows(mixed_qk[:, 1]), HV // HK, axis=1)
    gates_in = stored(jnp.dot(hidden_in, w_ba.reshape(D, 2 * HV), preferred_element_type=jnp.float32)).astype(jnp.float32).reshape(total_rows, 2, HV)
    strength = jax.nn.sigmoid(gates_in[:, 0] + beta_bias)
    log_decay = -jnp.exp(a_log) * jax.nn.softplus(gates_in[:, 1] + dt_bias)

    def token_step(current_state, inputs):
        query_vector, key_vector, value_row, beta_row, decay_row = inputs
        decayed_state = jnp.exp(decay_row)[:, None, None] * current_state
        predicted_value = jnp.einsum('xqf,xq->xf', decayed_state, key_vector, precision=exact_setting)
        written = beta_row[:, None] * (value_row - predicted_value)
        current_state = decayed_state + key_vector[:, :, None] * written[:, None, :]
        return (current_state, jnp.einsum('xqf,xq->xf', current_state, query_vector, precision=exact_setting))

    def block_step(current_state, block):
        current_state, outs = lax.scan(token_step, current_state, block)
        return (current_state, (outs, current_state))
    shaped = tuple((t.reshape((N_SEQ, TOK_DEV) + t.shape[1:]) for t in (queries, keys, values, strength, log_decay)))
    final_state, (outputs, checkpoints) = lax.scan(block_step, state_in.astype(jnp.float32), shaped)
    outputs = outputs.reshape(total_rows, HV, DV)
    gate_z = stored(jnp.dot(hidden_in, w_outgate, preferred_element_type=jnp.float32)).astype(jnp.float32).reshape(total_rows, HV, DV)
    scale = lax.rsqrt(lax.optimization_barrier(jnp.mean(outputs * outputs, axis=-1, keepdims=True)) + 1e-06)
    normed = (outputs * scale * norm_gain * jax.nn.silu(gate_z)).astype(jnp.bfloat16).reshape(total_rows, VALW)
    group = VALW // N_HEAD
    total = jnp.zeros((total_rows, D), jnp.float32)
    for member in range(N_HEAD):
        piece = jnp.dot(normed[:, member * group:(member + 1) * group], w_out[member * group:(member + 1) * group], preferred_element_type=jnp.float32)
        total = total + lax.optimization_barrier(piece.astype(jnp.bfloat16)).astype(jnp.float32)
    return (total.astype(jnp.bfloat16), checkpoints)
```

```python
import jax
import jax.numpy as jnp
from jax import lax
from jax.sharding import PartitionSpec as P

KEY_HEAD_SIZE = 128
DV = 128
SPAN = 64


exact_setting = lax.Precision.HIGHEST


def shifted(value, axis, steps):
    count = lax.axis_size(axis)
    leading, last = (max(0, -steps), min(count, count - steps))
    return lax.ppermute(value, axis, [(source, source + steps) for source in range(leading, last)])


def stored(values):
    return lax.optimization_barrier(values.astype(jnp.bfloat16))


def unit_rows(values):
    return values * lax.rsqrt(jnp.sum(values * values, axis=-1, keepdims=True) + 1e-06)


def causal_filter(history, present, weight):
    joined = jnp.concatenate([history, present], 0).astype(jnp.float32)
    count = present.shape[0]
    total = jnp.zeros(present.shape, jnp.float32)
    for offset in range(weight.shape[0]):
        total = total + weight[offset].astype(jnp.float32) * joined[offset : offset + count]
    return jax.nn.silu(total)


def mat_batch(left, right):
    return jnp.einsum("hij,hjk->hik", left, right, precision=exact_setting)


def to_front(values):
    return jnp.moveaxis(values, 1, 0)


def local(
    hidden_in,
    w_qk,
    w_value,
    w_outgate,
    w_ba,
    conv_qk,
    conv_value,
    hist_qk,
    hist_value,
    a_log,
    dt_bias,
    beta_bias,
    state_in,
    norm_gain,
    w_out,
):
    num_rows, model_width = hidden_in.shape
    key_cols = w_qk.shape[2]
    heads = a_log.shape[0]
    key_heads = key_cols // KEY_HEAD_SIZE
    taps = conv_value.shape[0]
    qk_flat = w_qk.reshape(model_width, 2 * key_cols)
    pre_qk = stored(jnp.dot(hidden_in, qk_flat, preferred_element_type=jnp.float32))
    pre_value = stored(jnp.dot(hidden_in, w_value, preferred_element_type=jnp.float32))
    rim_start = num_rows - (taps - 1)
    packed = jnp.concatenate([pre_qk[rim_start:], pre_value[rim_start:]], 1)
    moved = shifted(packed, "seq", 1)
    prev_qk = moved[:, : 2 * key_cols]
    prev_value = moved[:, 2 * key_cols :]
    leading = lax.axis_index("seq") == 0
    prev_qk = jnp.where(leading, hist_qk.reshape(taps - 1, 2 * key_cols), prev_qk)
    prev_value = jnp.where(leading, hist_value, prev_value)
    mixed_qk = causal_filter(prev_qk, pre_qk, conv_qk.reshape(taps, 2 * key_cols)).reshape(
        num_rows, 2, key_heads, KEY_HEAD_SIZE
    )
    values = causal_filter(prev_value, pre_value, conv_value).reshape(num_rows, heads, DV)
    ratio = heads // key_heads
    queries = jnp.repeat(unit_rows(mixed_qk[:, 0]) * KEY_HEAD_SIZE ** (-0.5), ratio, axis=1)
    keys = jnp.repeat(unit_rows(mixed_qk[:, 1]), ratio, axis=1)
    gates_in = (
        stored(
            jnp.dot(
                hidden_in, w_ba.reshape(model_width, 2 * heads), preferred_element_type=jnp.float32
            )
        )
        .astype(jnp.float32)
        .reshape(num_rows, 2, heads)
    )
    strength = jax.nn.sigmoid(gates_in[:, 0] + beta_bias)
    log_decay = -jnp.exp(a_log) * jax.nn.softplus(gates_in[:, 1] + dt_bias)
    blocks = num_rows // SPAN

    def spanned(values_in):
        return jnp.moveaxis(values_in, 1, 0).reshape((heads, blocks, SPAN) + values_in.shape[2:])

    query_c = spanned(queries)
    key_c = spanned(keys)
    value_c = spanned(values)
    beta_c = spanned(strength)
    cumul = jnp.cumsum(spanned(log_decay), axis=-1)
    spread = cumul[..., :, None] - cumul[..., None, :]
    places = jnp.arange(SPAN)
    below = places[:, None] > places[None, :]
    within = places[:, None] >= places[None, :]
    key_dots = jnp.einsum("hnid,hnjd->hnij", key_c, key_c, precision=exact_setting)
    lower_mat = (
        beta_c[..., :, None]
        * jnp.where(below, jnp.exp(jnp.where(below, spread, 0.0)), 0.0)
        * key_dots
    )
    identity_c = jnp.eye(SPAN, dtype=jnp.float32)
    power = lower_mat
    inverse = identity_c - lower_mat
    reach = 1
    while 2 * reach < SPAN:
        power = jnp.einsum("hnij,hnjk->hnik", power, power, precision=exact_setting)
        inverse = jnp.einsum(
            "hnij,hnjk->hnik", inverse, identity_c + power, precision=exact_setting
        )
        reach = reach * 2
    updates = jnp.einsum(
        "hnij,hnjv->hniv", inverse, beta_c[..., None] * value_c, precision=exact_setting
    )
    weights_k = jnp.einsum(
        "hnij,hnjk->hnik",
        inverse,
        (beta_c * jnp.exp(cumul))[..., None] * key_c,
        precision=exact_setting,
    )
    query_dots = jnp.einsum("hnid,hnjd->hnij", query_c, key_c, precision=exact_setting)
    attend = jnp.where(within, jnp.exp(jnp.where(within, spread, 0.0)), 0.0) * query_dots
    query_scaled = jnp.exp(cumul)[..., None] * query_c
    key_end = jnp.exp(cumul[..., -1:] - cumul)[..., None] * key_c
    block_fade = jnp.exp(cumul[..., -1])
    updates_aug = jnp.concatenate(
        [jnp.zeros((heads, blocks, SPAN, KEY_HEAD_SIZE), jnp.float32), updates], -1
    )
    eye_keys = jnp.broadcast_to(
        jnp.eye(KEY_HEAD_SIZE, dtype=jnp.float32), (heads, KEY_HEAD_SIZE, KEY_HEAD_SIZE)
    )
    start_aug = jnp.concatenate([eye_keys, jnp.zeros((heads, KEY_HEAD_SIZE, DV), jnp.float32)], -1)

    def advance(current_state, inputs):
        upd, wgt, qsc, att, kend, fade = inputs
        written = upd - jnp.einsum("hck,hkw->hcw", wgt, current_state, precision=exact_setting)
        readout = jnp.einsum(
            "hck,hkw->hcw", qsc, current_state, precision=exact_setting
        ) + jnp.einsum("hij,hjw->hiw", att, written, precision=exact_setting)
        current_state = fade[:, None, None] * current_state + jnp.einsum(
            "hck,hcw->hkw", kend, written, precision=exact_setting
        )
        return (current_state, readout)

    final_aug, readout_rows = lax.scan(
        advance,
        start_aug,
        (
            to_front(updates_aug),
            to_front(weights_k),
            to_front(query_scaled),
            to_front(attend),
            to_front(key_end),
            to_front(block_fade),
        ),
    )
    readout_rows = jnp.moveaxis(readout_rows, 0, 1).reshape(heads, num_rows, KEY_HEAD_SIZE + DV)
    carry_map = final_aug[..., :KEY_HEAD_SIZE]
    carry_add = final_aug[..., KEY_HEAD_SIZE:]

    span_add = jnp.where(leading, mat_batch(carry_map, state_in) + carry_add, carry_add)
    span_map = jnp.where(leading, 0.0, carry_map)
    count = lax.axis_size("seq")
    reach = 1
    while 2 * reach < count:
        both = jnp.concatenate([span_map, span_add], -1).astype(jnp.bfloat16)
        came = shifted(both, "seq", reach).astype(jnp.float32)
        joined = mat_batch(span_map, came)
        has_left = lax.axis_index("seq") >= reach
        span_add = joined[..., KEY_HEAD_SIZE:] + span_add
        span_map = jnp.where(has_left, joined[..., :KEY_HEAD_SIZE], span_map)
        reach = reach * 2
    came = shifted(span_add.astype(jnp.bfloat16), "seq", reach).astype(jnp.float32)
    span_add = mat_batch(span_map, came) + span_add
    checkpoint = span_add[None]
    came = shifted(span_add.astype(jnp.bfloat16), "seq", 1).astype(jnp.float32)
    initial_state = jnp.where(leading, state_in, came)
    outputs = readout_rows[..., KEY_HEAD_SIZE:] + jnp.einsum(
        "xlb,xbg->xlg", readout_rows[..., :KEY_HEAD_SIZE], initial_state, precision=exact_setting
    )
    outputs = jnp.moveaxis(outputs, 0, 1)
    gate_z = (
        stored(jnp.dot(hidden_in, w_outgate, preferred_element_type=jnp.float32))
        .astype(jnp.float32)
        .reshape(num_rows, heads, DV)
    )
    scale = lax.rsqrt(jnp.mean(outputs * outputs, axis=-1, keepdims=True) + 1e-06)
    normed = (
        (outputs * scale * norm_gain * jax.nn.silu(gate_z))
        .astype(jnp.bfloat16)
        .reshape(num_rows, heads * DV)
    )
    partial_out = jnp.dot(normed, w_out, preferred_element_type=jnp.float32)
    groups = lax.axis_size("head")
    terms = partial_out.astype(jnp.bfloat16).reshape(num_rows, groups, -1)
    terms = lax.all_to_all(terms, "head", 1, 0, tiled=False)
    mixed = jnp.sum(terms.astype(jnp.float32), axis=0).astype(jnp.bfloat16)
    return (mixed, checkpoint)


def solution(mesh):
    return jax.shard_map(
        local,
        mesh=mesh,
        in_specs=(
            P("seq", None),
            P(None, None, "head"),
            P(None, "head"),
            P(None, "head"),
            P(None, None, "head"),
            P(None, None, "head"),
            P(None, "head"),
            P(None, None, "head"),
            P(None, "head"),
            P("head"),
            P("head"),
            P("head"),
            P("head", None, None),
            P(),
            P("head", None),
        ),
        out_specs=(P("seq", "head"), P("seq", "head", None, None)),
        check_vma=False,
    )
```

```python
import functools

import jax
import jax.numpy as jnp
from jax import lax
from jax.experimental import pallas as pl
from jax.experimental.pallas import tpu as pltpu
from jax.sharding import PartitionSpec as P

KEY_HEAD_SIZE = 128
DV = 128
SPAN = 128
EDGE = 8


exact_setting = lax.Precision.HIGHEST


def half(values):
    return values.astype(jnp.bfloat16)


def mm(left, right, dims=((1,), (0,))):
    return lax.dot_general(half(left), half(right), (dims, ((), ())), preferred_element_type=jnp.float32)


def silu(values):
    return values / (1.0 + jnp.exp(-values))


def shifted(value, axis, steps):
    count = lax.axis_size(axis)
    leading, last = (max(0, -steps), min(count, count - steps))
    return lax.ppermute(value, axis, [(source, source + steps) for source in range(leading, last)])


def stored(values):
    return lax.optimization_barrier(values.astype(jnp.bfloat16))


def mat_batch(left, right):
    return jnp.einsum("hij,hjk->hik", left, right, precision=exact_setting)


def filtered(rim_ref, present_ref, weight_ref, room):
    count, width = present_ref.shape
    taps = weight_ref.shape[0]
    room[:EDGE, :width] = rim_ref[...].astype(jnp.float32)
    room[EDGE:, :width] = present_ref[...].astype(jnp.float32)
    first = EDGE - (taps - 1)
    total = jnp.zeros((count, width), jnp.float32)
    for tap in range(taps):
        weight = weight_ref[tap : tap + 1, :].astype(jnp.float32)
        total = total + weight * room[first + tap : first + tap + count, :width]
    return silu(total)


def unit_rows(values):
    return values * lax.rsqrt(jnp.sum(values * values, axis=-1, keepdims=True) + 1e-06)


def unit_inverses(lowers, row, col):
    size = row.shape[0]
    eye = jnp.where(row == col, 1.0, 0.0)
    step = 1
    results = None
    while step < size:
        pair = jnp.logical_and(row // (2 * step) == col // (2 * step), row // step > col // step)
        cross = [jnp.where(pair, lower, 0.0) for lower in lowers]
        if results is None:
            results = [eye - c for c in cross]
        else:
            inner = [mm(c, x) for c, x in zip(cross, results)]
            results = [x - mm(x, y) for x, y in zip(results, inner)]
        step = 2 * step
    return results


def block_kernel(
    q_rim, q_new, q_taps, k_rim, k_new, k_taps, v_rim, v_new, v_taps,
    beta_ref, cumul_ref, turned_ref, maps_ref, base_ref, slope_ref, room,
):
    queries = unit_rows(filtered(q_rim, q_new, q_taps, room)) * KEY_HEAD_SIZE ** (-0.5)
    keys = unit_rows(filtered(k_rim, k_new, k_taps, room))
    values = filtered(v_rim, v_new, v_taps, room)
    count = queries.shape[0]
    ratio = values.shape[1] // DV
    blocks = count // SPAN
    row = lax.broadcasted_iota(jnp.int32, (SPAN, SPAN), 0)
    col = lax.broadcasted_iota(jnp.int32, (SPAN, SPAN), 1)
    jobs = []
    for n in range(blocks):
        rows = slice(n * SPAN, (n + 1) * SPAN)
        query, key = queries[rows], keys[rows]
        key_dots = mm(key, key, ((1,), (1,)))
        query_dots = mm(query, key, ((1,), (1,)))
        for h in range(ratio):
            beta = beta_ref[0, rows, h : h + 1]
            cumul = cumul_ref[0, rows, h : h + 1]
            turned = turned_ref[0, h : h + 1, rows]
            last = turned[:, SPAN - 1 :]
            fading = jnp.exp(jnp.where(row >= col, cumul - turned, 0.0))
            grown = jnp.exp(cumul)
            jobs.append(
                dict(
                    n=n,
                    h=h,
                    rows=rows,
                    lower=jnp.where(row > col, beta * fading * key_dots, 0.0),
                    attend=jnp.where(row >= col, fading * query_dots, 0.0),
                    sides=jnp.concatenate(
                        [beta * grown * key, beta * values[rows, h * DV : (h + 1) * DV]], 1
                    ),
                    query=grown * query,
                    key_end=jnp.exp(last - cumul) * key,
                    fade=jnp.exp(last),
                )
            )
    inverses = unit_inverses([job["lower"] for job in jobs], row, col)
    solved = [mm(inverse, job["sides"]) for inverse, job in zip(inverses, jobs)]
    eye = jnp.where(row == col, 1.0, 0.0)
    none = jnp.zeros((SPAN, DV), jnp.float32)
    state = [None] * ratio
    for job, both in zip(jobs, solved):
        h, rows = job["h"], job["rows"]
        weights, updates = both[:, :KEY_HEAD_SIZE], both[:, KEY_HEAD_SIZE:]
        if job["n"] == 0:
            written = jnp.concatenate([-weights, updates], 1)
            seen = jnp.concatenate([job["query"], none], 1)
            carried = jnp.concatenate([job["fade"] * eye, none], 1)
        else:
            through = mm(jnp.concatenate([weights, job["query"]], 0), state[h])
            written = jnp.concatenate([none, updates], 1) - through[:SPAN]
            seen = through[SPAN:]
            carried = job["fade"] * state[h]
        readout = seen + mm(job["attend"], written)
        state[h] = carried + mm(job["key_end"], written, ((0,), (0,)))
        slope_ref[h, rows, :] = half(readout[:, :KEY_HEAD_SIZE])
        base_ref[h, rows, :] = readout[:, KEY_HEAD_SIZE:]
    for h in range(ratio):
        maps_ref[h] = state[h]


def block_maps(rim_qk, pre_qk, conv_qk, rim_value, pre_value, conv_value, beta, cumul):
    count = pre_qk.shape[0]
    key_heads = pre_qk.shape[1] // (2 * KEY_HEAD_SIZE)
    heads = pre_value.shape[1] // DV
    ratio = heads // key_heads
    taps = conv_qk.shape[0]
    wide = ratio * DV
    place = (lambda i: (0, i), lambda i: (0, key_heads + i), lambda i: (0, i))
    width = (KEY_HEAD_SIZE, KEY_HEAD_SIZE, wide)
    specs = []
    for at, size in zip(place, width):
        specs += [pl.BlockSpec((tall, size), at) for tall in (EDGE, count, taps)]
    paired = lambda a: jnp.moveaxis(a.reshape(count, key_heads, ratio), 1, 0)
    turned = jnp.moveaxis(cumul.reshape(count, key_heads, ratio), 0, 2)
    whole = lambda i: (i, 0, 0)
    return pl.pallas_call(
        block_kernel,
        grid=(key_heads,),
        in_specs=specs
        + [
            pl.BlockSpec((1, count, ratio), whole),
            pl.BlockSpec((1, count, ratio), whole),
            pl.BlockSpec((1, ratio, count), whole),
        ],
        out_specs=[
            pl.BlockSpec((ratio, KEY_HEAD_SIZE, KEY_HEAD_SIZE + DV), whole),
            pl.BlockSpec((ratio, count, DV), whole),
            pl.BlockSpec((ratio, count, KEY_HEAD_SIZE), whole),
        ],
        out_shape=[
            jax.ShapeDtypeStruct((heads, KEY_HEAD_SIZE, KEY_HEAD_SIZE + DV), jnp.float32),
            jax.ShapeDtypeStruct((heads, count, DV), jnp.float32),
            jax.ShapeDtypeStruct((heads, count, KEY_HEAD_SIZE), jnp.bfloat16),
        ],
        scratch_shapes=[pltpu.VMEM((EDGE + count, wide), jnp.float32)],
    )(
        rim_qk, pre_qk, conv_qk, rim_qk, pre_qk, conv_qk, rim_value, pre_value, conv_value,
        paired(beta), paired(cumul), turned,
    )


def finish_kernel(base_ref, slope_ref, state_ref, gate_ref, gain_ref, w_ref, out_ref):
    pieces = []
    for h in range(base_ref.shape[0]):
        gate = gate_ref[:, h * DV : (h + 1) * DV].astype(jnp.float32)
        output = base_ref[h] + mm(slope_ref[h], state_ref[h])
        scale = lax.rsqrt(jnp.mean(output * output, axis=-1, keepdims=True) + 1e-06)
        pieces.append(half(output * scale * gain_ref[...] * silu(gate)))
    normed = jnp.concatenate(pieces, 1)
    wide = out_ref.shape[2]
    for g in range(out_ref.shape[0]):
        out_ref[g] = half(mm(normed, w_ref[:, g * wide : (g + 1) * wide]))


def finish(base, slope, state, gate_z, norm_gain, w_out, groups):
    count, model_width = gate_z.shape[0], w_out.shape[1]
    return pl.pallas_call(
        finish_kernel,
        out_shape=jax.ShapeDtypeStruct((groups, count, model_width // groups), jnp.bfloat16),
    )(base, slope, state, gate_z, norm_gain.reshape(1, -1), w_out)


def local(
    hidden_in,
    w_qk,
    w_value,
    w_outgate,
    w_ba,
    conv_qk,
    conv_value,
    hist_qk,
    hist_value,
    a_log,
    dt_bias,
    beta_bias,
    state_in,
    norm_gain,
    w_out,
):
    num_rows, model_width = hidden_in.shape
    key_cols = w_qk.shape[2]
    heads = a_log.shape[0]
    taps = conv_value.shape[0]
    leading = lax.axis_index("seq") == 0
    edge_rows = shifted(hidden_in[num_rows - EDGE :], "seq", 1)
    qk_flat = w_qk.reshape(model_width, 2 * key_cols)
    pre_qk = stored(jnp.dot(hidden_in, qk_flat, preferred_element_type=jnp.float32))
    pre_value = stored(jnp.dot(hidden_in, w_value, preferred_element_type=jnp.float32))
    rim_qk = stored(jnp.dot(edge_rows, qk_flat, preferred_element_type=jnp.float32))
    rim_value = stored(jnp.dot(edge_rows, w_value, preferred_element_type=jnp.float32))
    pad = ((EDGE - (taps - 1), 0), (0, 0))
    rim_qk = jnp.where(leading, jnp.pad(hist_qk.reshape(taps - 1, 2 * key_cols), pad), rim_qk)
    rim_value = jnp.where(leading, jnp.pad(hist_value, pad), rim_value)
    gates_in = (
        stored(
            jnp.dot(
                hidden_in, w_ba.reshape(model_width, 2 * heads), preferred_element_type=jnp.float32
            )
        )
        .astype(jnp.float32)
        .reshape(num_rows, 2, heads)
    )
    strength = jax.nn.sigmoid(gates_in[:, 0] + beta_bias)
    log_decay = -jnp.exp(a_log) * jax.nn.softplus(gates_in[:, 1] + dt_bias)
    tokens = jnp.arange(num_rows)
    before = jnp.logical_and(
        tokens[:, None] >= tokens[None, :], tokens[:, None] // SPAN == tokens[None, :] // SPAN
    ).astype(jnp.float32)
    cumul = jnp.dot(before, log_decay, precision=exact_setting)
    maps, base, slope = block_maps(
        rim_qk, pre_qk, conv_qk.reshape(taps, 2 * key_cols),
        rim_value, pre_value, conv_value, strength, cumul,
    )
    carry_map = maps[..., :KEY_HEAD_SIZE]
    carry_add = maps[..., KEY_HEAD_SIZE:]
    gate_z = stored(jnp.dot(hidden_in, w_outgate, preferred_element_type=jnp.float32))
    span_add = jnp.where(leading, mat_batch(carry_map, state_in) + carry_add, carry_add)
    span_map = jnp.where(leading, 0.0, carry_map)
    count = lax.axis_size("seq")
    reach = 1
    while 2 * reach < count:
        both = jnp.concatenate([span_map, span_add], -1).astype(jnp.bfloat16)
        came = shifted(both, "seq", reach).astype(jnp.float32)
        joined = mat_batch(span_map, came)
        has_left = lax.axis_index("seq") >= reach
        span_add = joined[..., KEY_HEAD_SIZE:] + span_add
        span_map = jnp.where(has_left, joined[..., :KEY_HEAD_SIZE], span_map)
        reach = reach * 2
    came = shifted(span_add.astype(jnp.bfloat16), "seq", reach).astype(jnp.float32)
    span_add = mat_batch(span_map, came) + span_add
    checkpoint = span_add[None]
    came = shifted(span_add.astype(jnp.bfloat16), "seq", 1).astype(jnp.float32)
    initial_state = jnp.where(leading, state_in, came)
    groups = lax.axis_size("head")
    terms = finish(base, slope, initial_state, gate_z, norm_gain, w_out, groups)
    terms = lax.all_to_all(terms, "head", 0, 0, tiled=False)
    mixed = jnp.sum(terms.astype(jnp.float32), axis=0).astype(jnp.bfloat16)
    return (mixed, checkpoint)


def solution(mesh):
    return jax.shard_map(
        local,
        mesh=mesh,
        in_specs=(
            P("seq", None),
            P(None, None, "head"),
            P(None, "head"),
            P(None, "head"),
            P(None, None, "head"),
            P(None, None, "head"),
            P(None, "head"),
            P(None, None, "head"),
            P(None, "head"),
            P("head"),
            P("head"),
            P("head"),
            P("head", None, None),
            P(),
            P("head", None),
        ),
        out_specs=(P("seq", "head"), P("seq", "head", None, None)),
        check_vma=False,
    )
```

```python
import functools

import jax
import jax.numpy as jnp
from jax import lax
from jax.experimental import pallas as pl
from jax.experimental.pallas import tpu as pltpu
from jax.sharding import PartitionSpec as P

KEY_HEAD_SIZE = 128
DV = 128
SPAN = 128
EDGE = 8


exact_setting = lax.Precision.HIGHEST


def half(values):
    return values.astype(jnp.bfloat16)


def mm(left, right, dims=((1,), (0,))):
    return lax.dot_general(half(left), half(right), (dims, ((), ())), preferred_element_type=jnp.float32)


def silu(values):
    return values / (1.0 + jnp.exp(-values))


def shifted(value, axis, steps):
    count = lax.axis_size(axis)
    leading, last = (max(0, -steps), min(count, count - steps))
    return lax.ppermute(value, axis, [(source, source + steps) for source in range(leading, last)])


def stored(values):
    return lax.optimization_barrier(values.astype(jnp.bfloat16))


def filtered(rim_ref, present_ref, weight_ref, room):
    count, width = present_ref.shape
    taps = weight_ref.shape[0]
    room[:EDGE, :width] = rim_ref[...].astype(jnp.float32)
    room[EDGE:, :width] = present_ref[...].astype(jnp.float32)
    first = EDGE - (taps - 1)
    total = jnp.zeros((count, width), jnp.float32)
    for tap in range(taps):
        weight = weight_ref[tap : tap + 1, :].astype(jnp.float32)
        total = total + weight * room[first + tap : first + tap + count, :width]
    return silu(total)


def unit_rows(values):
    return values * lax.rsqrt(jnp.sum(values * values, axis=-1, keepdims=True) + 1e-06)


def unit_inverses(lowers, row, col):
    size = row.shape[0]
    eye = jnp.where(row == col, 1.0, 0.0)
    step = 1
    results = None
    while step < size:
        pair = jnp.logical_and(row // (2 * step) == col // (2 * step), row // step > col // step)
        cross = [jnp.where(pair, lower, 0.0) for lower in lowers]
        if results is None:
            results = [eye - c for c in cross]
        else:
            inner = [mm(c, x) for c, x in zip(cross, results)]
            results = [x - mm(x, y) for x, y in zip(results, inner)]
        step = 2 * step
    return results


def block_kernel(
    q_rim, q_new, q_taps, k_rim, k_new, k_taps, v_rim, v_new, v_taps,
    beta_ref, cumul_ref, turned_ref, maps_ref, base_ref, slope_ref, room,
):
    queries = unit_rows(filtered(q_rim, q_new, q_taps, room)) * KEY_HEAD_SIZE ** (-0.5)
    keys = unit_rows(filtered(k_rim, k_new, k_taps, room))
    values = filtered(v_rim, v_new, v_taps, room)
    count = queries.shape[0]
    ratio = values.shape[1] // DV
    blocks = count // SPAN
    row = lax.broadcasted_iota(jnp.int32, (SPAN, SPAN), 0)
    col = lax.broadcasted_iota(jnp.int32, (SPAN, SPAN), 1)
    jobs = []
    for n in range(blocks):
        rows = slice(n * SPAN, (n + 1) * SPAN)
        query, key = queries[rows], keys[rows]
        key_dots = mm(key, key, ((1,), (1,)))
        query_dots = mm(query, key, ((1,), (1,)))
        for h in range(ratio):
            beta = beta_ref[0, rows, h : h + 1]
            cumul = cumul_ref[0, rows, h : h + 1]
            turned = turned_ref[0, h : h + 1, rows]
            last = turned[:, SPAN - 1 :]
            fading = jnp.exp(jnp.where(row >= col, cumul - turned, 0.0))
            grown = jnp.exp(cumul)
            jobs.append(
                dict(
                    n=n,
                    h=h,
                    rows=rows,
                    lower=jnp.where(row > col, beta * fading * key_dots, 0.0),
                    attend=jnp.where(row >= col, fading * query_dots, 0.0),
                    sides=jnp.concatenate(
                        [beta * grown * key, beta * values[rows, h * DV : (h + 1) * DV]], 1
                    ),
                    query=grown * query,
                    key_end=jnp.exp(last - cumul) * key,
                    fade=jnp.exp(last),
                )
            )
    inverses = unit_inverses([job["lower"] for job in jobs], row, col)
    solved = [mm(inverse, job["sides"]) for inverse, job in zip(inverses, jobs)]
    eye = jnp.where(row == col, 1.0, 0.0)
    none = jnp.zeros((SPAN, DV), jnp.float32)
    state = [None] * ratio
    for job, both in zip(jobs, solved):
        h, rows = job["h"], job["rows"]
        weights, updates = both[:, :KEY_HEAD_SIZE], both[:, KEY_HEAD_SIZE:]
        if job["n"] == 0:
            written = jnp.concatenate([-weights, updates], 1)
            seen = jnp.concatenate([job["query"], none], 1)
            carried = jnp.concatenate([job["fade"] * eye, none], 1)
        else:
            through = mm(jnp.concatenate([weights, job["query"]], 0), state[h])
            written = jnp.concatenate([none, updates], 1) - through[:SPAN]
            seen = through[SPAN:]
            carried = job["fade"] * state[h]
        readout = seen + mm(job["attend"], written)
        state[h] = carried + mm(job["key_end"], written, ((0,), (0,)))
        slope_ref[h, rows, :] = half(readout[:, :KEY_HEAD_SIZE])
        base_ref[h, rows, :] = readout[:, KEY_HEAD_SIZE:]
    for h in range(ratio):
        maps_ref[h] = state[h]


def block_maps(rim_qk, pre_qk, conv_qk, rim_value, pre_value, conv_value, beta, cumul):
    count = pre_qk.shape[0]
    key_heads = pre_qk.shape[1] // (2 * KEY_HEAD_SIZE)
    heads = pre_value.shape[1] // DV
    ratio = heads // key_heads
    taps = conv_qk.shape[0]
    wide = ratio * DV
    place = (lambda i: (0, i), lambda i: (0, key_heads + i), lambda i: (0, i))
    width = (KEY_HEAD_SIZE, KEY_HEAD_SIZE, wide)
    specs = []
    for at, size in zip(place, width):
        specs += [pl.BlockSpec((tall, size), at) for tall in (EDGE, count, taps)]
    paired = lambda a: jnp.moveaxis(a.reshape(count, key_heads, ratio), 1, 0)
    turned = jnp.moveaxis(cumul.reshape(count, key_heads, ratio), 0, 2)
    whole = lambda i: (i, 0, 0)
    return pl.pallas_call(
        block_kernel,
        grid=(key_heads,),
        in_specs=specs
        + [
            pl.BlockSpec((1, count, ratio), whole),
            pl.BlockSpec((1, count, ratio), whole),
            pl.BlockSpec((1, ratio, count), whole),
        ],
        out_specs=[
            pl.BlockSpec((ratio, KEY_HEAD_SIZE, KEY_HEAD_SIZE + DV), whole),
            pl.BlockSpec((ratio, count, DV), whole),
            pl.BlockSpec((ratio, count, KEY_HEAD_SIZE), whole),
        ],
        out_shape=[
            jax.ShapeDtypeStruct((heads, KEY_HEAD_SIZE, KEY_HEAD_SIZE + DV), jnp.float32),
            jax.ShapeDtypeStruct((heads, count, DV), jnp.float32),
            jax.ShapeDtypeStruct((heads, count, KEY_HEAD_SIZE), jnp.bfloat16),
        ],
        scratch_shapes=[pltpu.VMEM((EDGE + count, wide), jnp.float32)],
    )(
        rim_qk, pre_qk, conv_qk, rim_qk, pre_qk, conv_qk, rim_value, pre_value, conv_value,
        paired(beta), paired(cumul), turned,
    )


def carry_kernel(
    maps_ref, base_ref, slope_ref, start_ref, gate_ref, gain_ref, w_ref, mixed_ref, check_ref,
    parts, gathered, before, states, hop_out, hop_in, terms, landed,
    part_send, part_recv, back_send, back_recv, hop_send, hop_recv, term_send, term_recv,
    *, count, groups,
):
    heads = maps_ref.shape[0]
    row = parts.shape[0]
    lines = count // row
    cut = row // heads
    tall = DV // cut
    place = lax.axis_index("seq")
    group = lax.axis_index("head")
    unit = lax.rem(place, row)
    line = place // row
    first = place - unit
    mesh_id = pl.DeviceIdType.MESH

    def mate(off):
        return lax.rem(unit + off, row)

    def peer(off):
        return lax.rem(group + off, groups)

    barrier = pltpu.get_barrier_semaphore()
    for off in range(1, row):
        pl.semaphore_signal(
            barrier, inc=1, device_id={"seq": first + mate(off)}, device_id_type=mesh_id
        )
    for step in (row, count - row):
        pl.semaphore_signal(
            barrier, inc=1, device_id={"seq": lax.rem(place + step, count)}, device_id_type=mesh_id
        )
    for off in range(1, groups):
        pl.semaphore_signal(barrier, inc=1, device_id={"head": peer(off)}, device_id_type=mesh_id)

    for h in range(heads):
        carry_map = half(maps_ref[h, :, :KEY_HEAD_SIZE])
        carry_add = half(maps_ref[h, :, KEY_HEAD_SIZE:].T)
        for c in range(cut):
            parts[h * cut + c, :KEY_HEAD_SIZE, :] = carry_map
            parts[h * cut + c, KEY_HEAD_SIZE:, :] = carry_add[c * tall : (c + 1) * tall]
    pl.semaphore_wait(barrier, (row - 1) + 2 + (groups - 1))

    def part_copy(off):
        return pltpu.make_async_remote_copy(
            src_ref=parts.at[mate(off)],
            dst_ref=gathered.at[unit],
            send_sem=part_send.at[off],
            recv_sem=part_recv.at[off],
            device_id={"seq": first + mate(off)},
            device_id_type=mesh_id,
        )

    moving = [part_copy(off) for off in range(1, row)]
    for copy in moving:
        copy.start()
    gathered[unit] = parts[unit]
    for h in range(heads):
        turned = start_ref[h].T
        for c in range(cut):

            @pl.when(unit == h * cut + c)
            def _():
                hop_out[...] = turned[c * tall : (c + 1) * tall]

    for copy in moving:
        copy.wait()

    hop = pltpu.make_async_remote_copy(
        src_ref=hop_out,
        dst_ref=hop_in,
        send_sem=hop_send,
        recv_sem=hop_recv,
        device_id={"seq": lax.rem(place + row, count)},
        device_id_type=mesh_id,
    )

    @pl.when(line > 0)
    def _():
        hop.wait_recv()
        hop_out[...] = hop_in[...]

    state = hop_out[...]
    for n in range(row):
        top = half(state)
        before[n] = top
        rest = half(state - top.astype(jnp.float32))
        both = mm(
            jnp.concatenate([top, rest], 0), gathered[n, :KEY_HEAD_SIZE, :], ((1,), (1,))
        )
        state = both[:tall] + both[tall:] + gathered[n, KEY_HEAD_SIZE:, :].astype(jnp.float32)
    hop_out[...] = state

    @pl.when(line < lines - 1)
    def _():
        hop.start()

    returning = [
        pltpu.make_async_remote_copy(
            src_ref=before.at[mate(off)],
            dst_ref=states.at[unit],
            send_sem=back_send.at[off],
            recv_sem=back_recv.at[off],
            device_id={"seq": first + mate(off)},
            device_id_type=mesh_id,
        )
        for off in range(1, row)
    ]
    for copy in returning:
        copy.start()
    states[unit] = before[unit]
    for copy in returning:
        copy.wait()

    pieces = []
    for h in range(heads):
        turned = jnp.concatenate([states[h * cut + c] for c in range(cut)], 0)
        gate = gate_ref[:, h * DV : (h + 1) * DV].astype(jnp.float32)
        output = base_ref[h] + mm(slope_ref[h], turned, ((1,), (1,)))
        scale = lax.rsqrt(jnp.mean(output * output, axis=-1, keepdims=True) + 1e-06)
        pieces.append(half(output * scale * gain_ref[...] * silu(gate)))
    normed = jnp.concatenate(pieces, 1)
    wide = mixed_ref.shape[1]

    def term(where):
        columns = pl.ds(pl.multiple_of(where * wide, wide), wide)
        return half(mm(normed, w_ref[:, columns]))

    leaving = []
    for off in range(1, groups):
        terms[off] = term(peer(off))
        copy = pltpu.make_async_remote_copy(
            src_ref=terms.at[off],
            dst_ref=landed.at[off],
            send_sem=term_send.at[off],
            recv_sem=term_recv.at[off],
            device_id={"head": peer(off)},
            device_id_type=mesh_id,
        )
        copy.start()
        leaving.append(copy)
    total = term(group).astype(jnp.float32)
    for h in range(heads):
        turned = jnp.concatenate([states[h * cut + c] for c in range(cut)], 0)
        check_ref[h] = (
            mm(maps_ref[h, :, :KEY_HEAD_SIZE], turned, ((1,), (1,)))
            + maps_ref[h, :, KEY_HEAD_SIZE:]
        )
    for off, copy in enumerate(leaving, 1):
        copy.wait()
        total = total + landed[off].astype(jnp.float32)
    mixed_ref[...] = half(total)

    @pl.when(line < lines - 1)
    def _():
        hop.wait_send()


def carry(maps, base, slope, state_in, gate_z, norm_gain, w_out):
    rows, model_width = gate_z.shape[0], w_out.shape[1]
    heads = maps.shape[0]
    count, groups = lax.axis_size("seq"), lax.axis_size("head")
    unit_count = min(2 * heads, count)
    tall = DV * heads // unit_count
    wide = model_width // groups
    dma = pltpu.SemaphoreType.DMA
    return pl.pallas_call(
        functools.partial(carry_kernel, count=count, groups=groups),
        out_shape=[
            jax.ShapeDtypeStruct((rows, wide), jnp.bfloat16),
            jax.ShapeDtypeStruct((heads, KEY_HEAD_SIZE, DV), jnp.float32),
        ],
        in_specs=[pl.BlockSpec(memory_space=pltpu.VMEM)] * 7,
        out_specs=[pl.BlockSpec(memory_space=pltpu.VMEM)] * 2,
        scratch_shapes=[
            pltpu.VMEM((unit_count, KEY_HEAD_SIZE + tall, KEY_HEAD_SIZE), jnp.bfloat16),
            pltpu.VMEM((unit_count, KEY_HEAD_SIZE + tall, KEY_HEAD_SIZE), jnp.bfloat16),
            pltpu.VMEM((unit_count, tall, KEY_HEAD_SIZE), jnp.bfloat16),
            pltpu.VMEM((unit_count, tall, KEY_HEAD_SIZE), jnp.bfloat16),
            pltpu.VMEM((tall, KEY_HEAD_SIZE), jnp.float32),
            pltpu.VMEM((tall, KEY_HEAD_SIZE), jnp.float32),
            pltpu.VMEM((groups, rows, wide), jnp.bfloat16),
            pltpu.VMEM((groups, rows, wide), jnp.bfloat16),
            dma((unit_count,)),
            dma((unit_count,)),
            dma((unit_count,)),
            dma((unit_count,)),
            dma(()),
            dma(()),
            dma((groups,)),
            dma((groups,)),
        ],
        compiler_params=pltpu.CompilerParams(
            collective_id=0, has_side_effects=True, vmem_limit_bytes=40 * 2**20
        ),
    )(maps, base, slope, state_in, gate_z, norm_gain.reshape(1, -1), w_out)


def local(
    hidden_in,
    w_qk,
    w_value,
    w_outgate,
    w_ba,
    conv_qk,
    conv_value,
    hist_qk,
    hist_value,
    a_log,
    dt_bias,
    beta_bias,
    state_in,
    norm_gain,
    w_out,
):
    num_rows, model_width = hidden_in.shape
    key_cols = w_qk.shape[2]
    heads = a_log.shape[0]
    taps = conv_value.shape[0]
    leading = lax.axis_index("seq") == 0
    edge_rows = shifted(hidden_in[num_rows - EDGE :], "seq", 1)
    qk_flat = w_qk.reshape(model_width, 2 * key_cols)
    pre_qk = stored(jnp.dot(hidden_in, qk_flat, preferred_element_type=jnp.float32))
    pre_value = stored(jnp.dot(hidden_in, w_value, preferred_element_type=jnp.float32))
    rim_qk = stored(jnp.dot(edge_rows, qk_flat, preferred_element_type=jnp.float32))
    rim_value = stored(jnp.dot(edge_rows, w_value, preferred_element_type=jnp.float32))
    pad = ((EDGE - (taps - 1), 0), (0, 0))
    rim_qk = jnp.where(leading, jnp.pad(hist_qk.reshape(taps - 1, 2 * key_cols), pad), rim_qk)
    rim_value = jnp.where(leading, jnp.pad(hist_value, pad), rim_value)
    gates_in = (
        stored(
            jnp.dot(
                hidden_in, w_ba.reshape(model_width, 2 * heads), preferred_element_type=jnp.float32
            )
        )
        .astype(jnp.float32)
        .reshape(num_rows, 2, heads)
    )
    strength = jax.nn.sigmoid(gates_in[:, 0] + beta_bias)
    log_decay = -jnp.exp(a_log) * jax.nn.softplus(gates_in[:, 1] + dt_bias)
    tokens = jnp.arange(num_rows)
    before = jnp.logical_and(
        tokens[:, None] >= tokens[None, :], tokens[:, None] // SPAN == tokens[None, :] // SPAN
    ).astype(jnp.float32)
    cumul = jnp.dot(before, log_decay, precision=exact_setting)
    maps, base, slope = block_maps(
        rim_qk, pre_qk, conv_qk.reshape(taps, 2 * key_cols),
        rim_value, pre_value, conv_value, strength, cumul,
    )
    gate_z = stored(jnp.dot(hidden_in, w_outgate, preferred_element_type=jnp.float32))
    mixed, checkpoint = carry(maps, base, slope, state_in, gate_z, norm_gain, w_out)
    return (mixed, checkpoint[None])


def solution(mesh):
    return jax.shard_map(
        local,
        mesh=mesh,
        in_specs=(
            P("seq", None),
            P(None, None, "head"),
            P(None, "head"),
            P(None, "head"),
            P(None, None, "head"),
            P(None, None, "head"),
            P(None, "head"),
            P(None, None, "head"),
            P(None, "head"),
            P("head"),
            P("head"),
            P("head"),
            P("head", None, None),
            P(),
            P("head", None),
        ),
        out_specs=(P("seq", "head"), P("seq", "head", None, None)),
        check_vma=False,
    )
```

```python
import functools

import jax
import jax.numpy as jnp
from jax import lax
from jax.experimental import pallas as pl
from jax.experimental.pallas import tpu as pltpu
from jax.sharding import PartitionSpec as P

KEY_HEAD_SIZE = 128
DV = 128
SPAN = 128
EDGE = 16
LANES = 128


exact_setting = lax.Precision.HIGHEST


def half(values):
    return values.astype(jnp.bfloat16)


def mm(left, right, dims=((1,), (0,))):
    return lax.dot_general(half(left), half(right), (dims, ((), ())), preferred_element_type=jnp.float32)


def silu(values):
    return values / (1.0 + jnp.exp(-values))


def stored(values):
    return lax.optimization_barrier(values.astype(jnp.bfloat16))


def filtered(room, weight_ref, columns, shift, begin, count):
    taps = weight_ref.shape[0]
    first = EDGE - (taps - 1) + begin
    wide = columns.stop - columns.start
    where = slice(columns.start + shift, columns.stop + shift)
    total = jnp.zeros((count, wide), jnp.float32)
    for tap in range(taps):
        weight = weight_ref[tap : tap + 1, columns].astype(jnp.float32)
        total = total + weight * room[first + tap : first + tap + count, where]
    return silu(total)


def unit_rows(values):
    return values * lax.rsqrt(jnp.sum(values * values, axis=-1, keepdims=True) + 1e-06)


def unit_inverses(lowers, row, col):
    size = row.shape[0]
    eye = jnp.where(row == col, 1.0, 0.0)
    step = 1
    results = None
    while step < size:
        pair = jnp.logical_and(row // (2 * step) == col // (2 * step), row // step > col // step)
        cross = [jnp.where(pair, lower, 0.0) for lower in lowers]
        if results is None:
            results = [eye - c for c in cross]
        else:
            inner = [mm(c, x) for c, x in zip(cross, results)]
            results = [x - mm(x, y) for x, y in zip(results, inner)]
        step = 2 * step
    return results


def layer_kernel(
    pre_qk, pre_value, taps_qk, taps_value, history, gates_ref, rows_ref, start_ref, gain_ref,
    hidden_hbm, gate_hbm, out_hbm, mixed_ref, check_ref,
    room, rim_qk, rim_value, maps_ref, base_ref, slope_ref, hidden, w_gate, w_ref,
    parts, gathered, before, states, hop_out, hop_in, terms, landed,
    fetch_sem, rim_send, rim_recv,
    part_send, part_recv, back_send, back_recv, hop_send, hop_recv, term_send, term_recv,
    *, count, groups,
):
    heads = maps_ref.shape[0]
    tokens = pre_qk.shape[0]
    key_cols = pre_qk.shape[1] // 2
    key_heads = key_cols // KEY_HEAD_SIZE
    ratio = heads // key_heads
    row = parts.shape[0]
    lines = count // row
    cut = row // heads
    tall = DV // cut
    place = lax.axis_index("seq")
    group = lax.axis_index("head")
    unit = lax.rem(place, row)
    line = place // row
    first = place - unit
    mesh_id = pl.DeviceIdType.MESH

    def mate(off):
        return lax.rem(unit + off, row)

    def peer(off):
        return lax.rem(group + off, groups)

    barrier = pltpu.get_barrier_semaphore()
    for step in (1, count - 1, row, count - row):
        pl.semaphore_signal(
            barrier, inc=1, device_id={"seq": lax.rem(place + step, count)}, device_id_type=mesh_id
        )
    for off in range(1, row):
        pl.semaphore_signal(
            barrier, inc=1, device_id={"seq": first + mate(off)}, device_id_type=mesh_id
        )
    for off in range(1, groups):
        pl.semaphore_signal(barrier, inc=1, device_id={"head": peer(off)}, device_id_type=mesh_id)

    fetches = [
        pltpu.make_async_copy(source, target, fetch_sem.at[i])
        for i, (source, target) in enumerate(
            ((hidden_hbm, hidden), (gate_hbm, w_gate), (out_hbm, w_ref))
        )
    ]
    for copy in fetches:
        copy.start()

    gates = gates_ref[...].astype(jnp.float32) + rows_ref[0:1, :]
    strength = 1.0 / (1.0 + jnp.exp(-gates))
    soft = jnp.maximum(gates, 0.0) + jnp.log1p(jnp.exp(-jnp.abs(gates)))
    log_decay = -jnp.exp(rows_ref[1:2, :]) * soft
    row_at = lax.broadcasted_iota(jnp.int32, (SPAN, SPAN), 0)
    col_at = lax.broadcasted_iota(jnp.int32, (SPAN, SPAN), 1)
    running = jnp.where(row_at >= col_at, 1.0, 0.0)
    eye = jnp.where(row_at == col_at, 1.0, 0.0)

    pl.semaphore_wait(barrier, 4 + (row - 1) + (groups - 1))
    rims = [
        pltpu.make_async_remote_copy(
            src_ref=source.at[pl.ds(tokens - EDGE, EDGE)],
            dst_ref=target,
            send_sem=rim_send.at[i],
            recv_sem=rim_recv.at[i],
            device_id={"seq": lax.rem(place + 1, count)},
            device_id_type=mesh_id,
        )
        for i, (source, target) in enumerate(((pre_qk, rim_qk), (pre_value, rim_value)))
    ]

    @pl.when(place < count - 1)
    def _():
        for copy in rims:
            copy.start()

    room[EDGE:, : 2 * key_cols] = pre_qk[...].astype(jnp.float32)
    room[EDGE:, 2 * key_cols :] = pre_value[...].astype(jnp.float32)

    def chunk(n):
        begin = n * SPAN
        rows = slice(begin, begin + SPAN)
        cumul_all = jnp.dot(running, log_decay[rows], precision=exact_setting)
        turned_all = cumul_all.T
        jobs = []
        for kh in range(key_heads):
            q_at = slice(kh * KEY_HEAD_SIZE, (kh + 1) * KEY_HEAD_SIZE)
            k_at = slice(key_cols + q_at.start, key_cols + q_at.stop)
            query = unit_rows(filtered(room, taps_qk, q_at, 0, begin, SPAN))
            query = query * KEY_HEAD_SIZE ** (-0.5)
            key = unit_rows(filtered(room, taps_qk, k_at, 0, begin, SPAN))
            key_dots = mm(key, key, ((1,), (1,)))
            query_dots = mm(query, key, ((1,), (1,)))
            for h in range(kh * ratio, (kh + 1) * ratio):
                v_at = slice(h * DV, (h + 1) * DV)
                value = filtered(room, taps_value, v_at, 2 * key_cols, begin, SPAN)
                beta = strength[rows, h : h + 1]
                cumul = cumul_all[:, heads + h : heads + h + 1]
                turned = turned_all[heads + h : heads + h + 1, :]
                last = turned[:, SPAN - 1 :]
                fading = jnp.exp(jnp.where(row_at >= col_at, cumul - turned, 0.0))
                grown = jnp.exp(cumul)
                jobs.append(
                    dict(
                        h=h,
                        lower=jnp.where(row_at > col_at, beta * fading * key_dots, 0.0),
                        attend=half(jnp.where(row_at >= col_at, fading * query_dots, 0.0)),
                        sides=half(jnp.concatenate([beta * grown * key, beta * value], 1)),
                        query=grown * query,
                        key_end=half(jnp.exp(last - cumul) * key),
                        fade=jnp.exp(last),
                    )
                )
        inverses = unit_inverses([job["lower"] for job in jobs], row_at, col_at)
        for job, inverse in zip(jobs, inverses):
            job["both"] = mm(inverse, job["sides"])
        return jobs

    blocks = tokens // SPAN
    prepared = {n: chunk(n) for n in range(1, blocks)}

    @pl.when(place > 0)
    def _():
        for copy in rims:
            copy.wait_recv()
        room[:EDGE, : 2 * key_cols] = rim_qk[...].astype(jnp.float32)
        room[:EDGE, 2 * key_cols :] = rim_value[...].astype(jnp.float32)

    @pl.when(place == 0)
    def _():
        room[:EDGE, :] = history[...].astype(jnp.float32)

    prepared[0] = chunk(0)
    none = jnp.zeros((SPAN, DV), jnp.float32)
    state = [None] * heads
    for n in range(blocks):
        rows = slice(n * SPAN, (n + 1) * SPAN)
        for job in prepared[n]:
            h, both = job["h"], job["both"]
            weights, updates = both[:, :KEY_HEAD_SIZE], both[:, KEY_HEAD_SIZE:]
            if n == 0:
                written = jnp.concatenate([-weights, updates], 1)
                seen = jnp.concatenate([job["query"], none], 1)
                carried = jnp.concatenate([job["fade"] * eye, none], 1)
            else:
                through = mm(jnp.concatenate([weights, job["query"]], 0), state[h])
                written = jnp.concatenate([none, updates], 1) - through[:SPAN]
                seen = through[SPAN:]
                carried = job["fade"] * state[h]
            readout = seen + mm(job["attend"], written)
            state[h] = carried + mm(job["key_end"], written, ((0,), (0,)))
            slope_ref[h, rows, :] = half(readout[:, :KEY_HEAD_SIZE])
            base_ref[h, rows, :] = readout[:, KEY_HEAD_SIZE:]
    for h in range(heads):
        maps_ref[h] = state[h]

    for h in range(heads):
        carry_map = half(maps_ref[h, :, :KEY_HEAD_SIZE])
        carry_add = half(maps_ref[h, :, KEY_HEAD_SIZE:].T)
        for c in range(cut):
            parts[h * cut + c, :KEY_HEAD_SIZE, :] = carry_map
            parts[h * cut + c, KEY_HEAD_SIZE:, :] = carry_add[c * tall : (c + 1) * tall]
    def part_copy(off):
        return pltpu.make_async_remote_copy(
            src_ref=parts.at[mate(off)],
            dst_ref=gathered.at[unit],
            send_sem=part_send.at[off],
            recv_sem=part_recv.at[off],
            device_id={"seq": first + mate(off)},
            device_id_type=mesh_id,
        )

    moving = [part_copy(off) for off in range(1, row)]
    for copy in moving:
        copy.start()
    gathered[unit] = parts[unit]
    for h in range(heads):
        turned = start_ref[h].T
        for c in range(cut):

            @pl.when(unit == h * cut + c)
            def _():
                hop_out[...] = turned[c * tall : (c + 1) * tall]

    for copy in fetches:
        copy.wait()
    gate_all = half(mm(hidden[...], w_gate[...])).astype(jnp.float32)
    for copy in moving:
        copy.wait()

    hop = pltpu.make_async_remote_copy(
        src_ref=hop_out,
        dst_ref=hop_in,
        send_sem=hop_send,
        recv_sem=hop_recv,
        device_id={"seq": lax.rem(place + row, count)},
        device_id_type=mesh_id,
    )

    @pl.when(line > 0)
    def _():
        hop.wait_recv()
        hop_out[...] = hop_in[...]

    state = hop_out[...]
    for n in range(row):
        top = half(state)
        before[n] = top
        rest = half(state - top.astype(jnp.float32))
        both = mm(
            jnp.concatenate([top, rest], 0), gathered[n, :KEY_HEAD_SIZE, :], ((1,), (1,))
        )
        state = both[:tall] + both[tall:] + gathered[n, KEY_HEAD_SIZE:, :].astype(jnp.float32)
    hop_out[...] = state

    @pl.when(line < lines - 1)
    def _():
        hop.start()

    returning = [
        pltpu.make_async_remote_copy(
            src_ref=before.at[mate(off)],
            dst_ref=states.at[unit],
            send_sem=back_send.at[off],
            recv_sem=back_recv.at[off],
            device_id={"seq": first + mate(off)},
            device_id_type=mesh_id,
        )
        for off in range(1, row)
    ]
    for copy in returning:
        copy.start()
    states[unit] = before[unit]
    for copy in returning:
        copy.wait()

    pieces = []
    for h in range(heads):
        turned = jnp.concatenate([states[h * cut + c] for c in range(cut)], 0)
        gate = gate_all[:, h * DV : (h + 1) * DV]
        output = base_ref[h] + mm(slope_ref[h], turned, ((1,), (1,)))
        scale = lax.rsqrt(jnp.mean(output * output, axis=-1, keepdims=True) + 1e-06)
        pieces.append(half(output * scale * gain_ref[...] * silu(gate)))
    normed = jnp.concatenate(pieces, 1)
    wide = mixed_ref.shape[1]

    def term(where):
        columns = pl.ds(pl.multiple_of(where * wide, wide), wide)
        return half(mm(normed, w_ref[:, columns]))

    leaving = []
    for off in range(1, groups):
        terms[off] = term(peer(off))
        copy = pltpu.make_async_remote_copy(
            src_ref=terms.at[off],
            dst_ref=landed.at[off],
            send_sem=term_send.at[off],
            recv_sem=term_recv.at[off],
            device_id={"head": peer(off)},
            device_id_type=mesh_id,
        )
        copy.start()
        leaving.append(copy)
    total = term(group).astype(jnp.float32)
    for h in range(heads):
        turned = jnp.concatenate([states[h * cut + c] for c in range(cut)], 0)
        check_ref[h] = (
            mm(maps_ref[h, :, :KEY_HEAD_SIZE], turned, ((1,), (1,)))
            + maps_ref[h, :, KEY_HEAD_SIZE:]
        )
    for off, copy in enumerate(leaving, 1):
        copy.wait()
        total = total + landed[off].astype(jnp.float32)
    mixed_ref[...] = half(total)

    @pl.when(line < lines - 1)
    def _():
        hop.wait_send()

    @pl.when(place < count - 1)
    def _():
        for copy in rims:
            copy.wait_send()


def layer(
    pre_qk, pre_value, taps_qk, taps_value, history, gates, rows, state_in, gain,
    hidden, w_gate, w_out,
):
    tokens, model_width = hidden.shape
    heads = state_in.shape[0]
    count, groups = lax.axis_size("seq"), lax.axis_size("head")
    unit_count = min(2 * heads, count)
    tall = DV * heads // unit_count
    wide = model_width // groups
    room_wide = pre_qk.shape[1] + pre_value.shape[1]
    dma = pltpu.SemaphoreType.DMA
    bf16, f32 = jnp.bfloat16, jnp.float32
    return pl.pallas_call(
        functools.partial(layer_kernel, count=count, groups=groups),
        out_shape=[
            jax.ShapeDtypeStruct((tokens, wide), bf16),
            jax.ShapeDtypeStruct((heads, KEY_HEAD_SIZE, DV), f32),
        ],
        in_specs=[pl.BlockSpec(memory_space=pltpu.VMEM)] * 9
        + [pl.BlockSpec(memory_space=pl.ANY)] * 3,
        out_specs=[pl.BlockSpec(memory_space=pltpu.VMEM)] * 2,
        scratch_shapes=[
            pltpu.VMEM((EDGE + tokens, room_wide), f32),
            pltpu.VMEM((EDGE, pre_qk.shape[1]), bf16),
            pltpu.VMEM((EDGE, pre_value.shape[1]), bf16),
            pltpu.VMEM((heads, KEY_HEAD_SIZE, KEY_HEAD_SIZE + DV), f32),
            pltpu.VMEM((heads, tokens, DV), f32),
            pltpu.VMEM((heads, tokens, KEY_HEAD_SIZE), bf16),
            pltpu.VMEM(hidden.shape, bf16),
            pltpu.VMEM(w_gate.shape, bf16),
            pltpu.VMEM(w_out.shape, bf16),
            pltpu.VMEM((unit_count, KEY_HEAD_SIZE + tall, KEY_HEAD_SIZE), bf16),
            pltpu.VMEM((unit_count, KEY_HEAD_SIZE + tall, KEY_HEAD_SIZE), bf16),
            pltpu.VMEM((unit_count, tall, KEY_HEAD_SIZE), bf16),
            pltpu.VMEM((unit_count, tall, KEY_HEAD_SIZE), bf16),
            pltpu.VMEM((tall, KEY_HEAD_SIZE), f32),
            pltpu.VMEM((tall, KEY_HEAD_SIZE), f32),
            pltpu.VMEM((groups, tokens, wide), bf16),
            pltpu.VMEM((groups, tokens, wide), bf16),
            dma((3,)),
            dma((2,)),
            dma((2,)),
            dma((unit_count,)),
            dma((unit_count,)),
            dma((unit_count,)),
            dma((unit_count,)),
            dma(()),
            dma(()),
            dma((groups,)),
            dma((groups,)),
        ],
        compiler_params=pltpu.CompilerParams(
            collective_id=0, has_side_effects=True, vmem_limit_bytes=40 * 2**20
        ),
    )(
        pre_qk, pre_value, taps_qk, taps_value, history, gates, rows, state_in, gain,
        hidden, w_gate, w_out,
    )


def local(
    hidden_in,
    w_qk,
    w_value,
    w_outgate,
    w_ba,
    conv_qk,
    conv_value,
    hist_qk,
    hist_value,
    a_log,
    dt_bias,
    beta_bias,
    state_in,
    norm_gain,
    w_out,
):
    num_rows, model_width = hidden_in.shape
    key_cols = w_qk.shape[2]
    heads = a_log.shape[0]
    taps = conv_value.shape[0]
    qk_flat = w_qk.reshape(model_width, 2 * key_cols)
    pre_qk = stored(jnp.dot(hidden_in, qk_flat, preferred_element_type=jnp.float32))
    pre_value = stored(jnp.dot(hidden_in, w_value, preferred_element_type=jnp.float32))
    w_gates = jnp.pad(w_ba.reshape(model_width, 2 * heads), ((0, 0), (0, LANES - 2 * heads)))
    gates = stored(jnp.dot(hidden_in, w_gates, preferred_element_type=jnp.float32))
    history = jnp.concatenate([hist_qk.reshape(taps - 1, 2 * key_cols), hist_value], 1)
    history = jnp.pad(history, ((EDGE - (taps - 1), 0), (0, 0)))
    unused = jnp.zeros((LANES - 2 * heads,), jnp.float32)
    rows = jnp.stack(
        [
            jnp.concatenate([beta_bias, dt_bias, unused]),
            jnp.concatenate([a_log, a_log, unused]),
        ]
    )
    mixed, checkpoint = layer(
        pre_qk, pre_value, conv_qk.reshape(taps, 2 * key_cols), conv_value, history, gates, rows,
        state_in, norm_gain.reshape(1, -1), hidden_in, w_outgate, w_out,
    )
    return (mixed, checkpoint[None])


def solution(mesh):
    return jax.shard_map(
        local,
        mesh=mesh,
        in_specs=(
            P("seq", None),
            P(None, None, "head"),
            P(None, "head"),
            P(None, "head"),
            P(None, None, "head"),
            P(None, None, "head"),
            P(None, "head"),
            P(None, None, "head"),
            P(None, "head"),
            P("head"),
            P("head"),
            P("head"),
            P("head", None, None),
            P(),
            P("head", None),
        ),
        out_specs=(P("seq", "head"), P("seq", "head", None, None)),
        check_vma=False,
    )
```

```python
import functools

import jax
import jax.numpy as jnp
from jax import lax
from jax.experimental import pallas as pl
from jax.experimental.pallas import tpu as pltpu
from jax.sharding import PartitionSpec as P

KEY_HEAD_SIZE = 128
DV = 128
SPAN = 128
EDGE = 16
LANES = 128


exact_setting = lax.Precision.HIGHEST


def half(values):
    return values.astype(jnp.bfloat16)


def mm(left, right, dims=((1,), (0,))):
    return lax.dot_general(half(left), half(right), (dims, ((), ())), preferred_element_type=jnp.float32)


def silu(values):
    return values / (1.0 + jnp.exp(-values))


def stored(values):
    return lax.optimization_barrier(values.astype(jnp.bfloat16))


def filtered(room, weight_ref, columns, shift, begin, count):
    taps = weight_ref.shape[0]
    first = EDGE - (taps - 1) + begin
    wide = columns.stop - columns.start
    where = slice(columns.start + shift, columns.stop + shift)
    total = jnp.zeros((count, wide), jnp.float32)
    for tap in range(taps):
        weight = weight_ref[tap : tap + 1, columns].astype(jnp.float32)
        total = total + weight * room[first + tap : first + tap + count, where]
    return silu(total)


def unit_rows(values):
    return values * lax.rsqrt(jnp.sum(values * values, axis=-1, keepdims=True) + 1e-06)


def unit_inverses(lowers, row, col):
    size = row.shape[0]
    eye = jnp.where(row == col, 1.0, 0.0)
    step = 1
    results = None
    while step < size:
        pair = jnp.logical_and(row // (2 * step) == col // (2 * step), row // step > col // step)
        cross = [jnp.where(pair, lower, 0.0) for lower in lowers]
        if results is None:
            results = [eye - c for c in cross]
        else:
            inner = [mm(c, x) for c, x in zip(cross, results)]
            results = [x - mm(x, y) for x, y in zip(results, inner)]
        step = 2 * step
    return results


def layer_kernel(
    pre_qk, pre_value, taps_qk, taps_value, history, gates_ref, rows_ref, start_ref, gain_ref,
    hidden_hbm, gate_hbm, out_hbm, mixed_ref, check_ref,
    room, rim_qk, rim_value, maps_ref, base_ref, slope_ref, hidden, w_gate, w_ref,
    parts, gathered, before, states, entry, hop_out, hop_in, terms, landed,
    fetch_sem, rim_send, rim_recv,
    part_send, part_recv, back_send, back_recv, hop_send, hop_recv, term_send, term_recv,
    *, count, groups,
):
    heads = maps_ref.shape[0]
    tokens = pre_qk.shape[0]
    key_cols = pre_qk.shape[1] // 2
    key_heads = key_cols // KEY_HEAD_SIZE
    ratio = heads // key_heads
    row = parts.shape[0]
    lines = count // row
    cut = row // heads
    tall = DV // cut
    place = lax.axis_index("seq")
    group = lax.axis_index("head")
    unit = lax.rem(place, row)
    line = place // row
    first = place - unit
    mesh_id = pl.DeviceIdType.MESH

    def mate(off):
        return lax.rem(unit + off, row)

    def peer(off):
        return lax.rem(group + off, groups)

    barrier = pltpu.get_barrier_semaphore()
    for step in (1, count - 1, row, count - row):
        pl.semaphore_signal(
            barrier, inc=1, device_id={"seq": lax.rem(place + step, count)}, device_id_type=mesh_id
        )
    for off in range(1, row):
        pl.semaphore_signal(
            barrier, inc=1, device_id={"seq": first + mate(off)}, device_id_type=mesh_id
        )
    for off in range(1, groups):
        pl.semaphore_signal(barrier, inc=1, device_id={"head": peer(off)}, device_id_type=mesh_id)

    fetches = [
        pltpu.make_async_copy(source, target, fetch_sem.at[i])
        for i, (source, target) in enumerate(
            ((hidden_hbm, hidden), (gate_hbm, w_gate), (out_hbm, w_ref))
        )
    ]
    for copy in fetches:
        copy.start()

    gates = gates_ref[...].astype(jnp.float32) + rows_ref[0:1, :]
    strength = 1.0 / (1.0 + jnp.exp(-gates))
    soft = jnp.maximum(gates, 0.0) + jnp.log1p(jnp.exp(-jnp.abs(gates)))
    log_decay = -jnp.exp(rows_ref[1:2, :]) * soft
    row_at = lax.broadcasted_iota(jnp.int32, (SPAN, SPAN), 0)
    col_at = lax.broadcasted_iota(jnp.int32, (SPAN, SPAN), 1)
    running = jnp.where(row_at >= col_at, 1.0, 0.0)
    eye = jnp.where(row_at == col_at, 1.0, 0.0)

    pl.semaphore_wait(barrier, 4 + (row - 1) + (groups - 1))
    rims = [
        pltpu.make_async_remote_copy(
            src_ref=source.at[pl.ds(tokens - EDGE, EDGE)],
            dst_ref=target,
            send_sem=rim_send.at[i],
            recv_sem=rim_recv.at[i],
            device_id={"seq": lax.rem(place + 1, count)},
            device_id_type=mesh_id,
        )
        for i, (source, target) in enumerate(((pre_qk, rim_qk), (pre_value, rim_value)))
    ]

    @pl.when(place < count - 1)
    def _():
        for copy in rims:
            copy.start()

    room[EDGE:, : 2 * key_cols] = pre_qk[...].astype(jnp.float32)
    room[EDGE:, 2 * key_cols :] = pre_value[...].astype(jnp.float32)

    def chunk(n):
        begin = n * SPAN
        rows = slice(begin, begin + SPAN)
        cumul_all = jnp.dot(running, log_decay[rows], precision=exact_setting)
        turned_all = cumul_all.T
        jobs = []
        for kh in range(key_heads):
            q_at = slice(kh * KEY_HEAD_SIZE, (kh + 1) * KEY_HEAD_SIZE)
            k_at = slice(key_cols + q_at.start, key_cols + q_at.stop)
            query = unit_rows(filtered(room, taps_qk, q_at, 0, begin, SPAN))
            query = query * KEY_HEAD_SIZE ** (-0.5)
            key = unit_rows(filtered(room, taps_qk, k_at, 0, begin, SPAN))
            key_dots = mm(key, key, ((1,), (1,)))
            query_dots = mm(query, key, ((1,), (1,)))
            for h in range(kh * ratio, (kh + 1) * ratio):
                v_at = slice(h * DV, (h + 1) * DV)
                value = filtered(room, taps_value, v_at, 2 * key_cols, begin, SPAN)
                beta = strength[rows, h : h + 1]
                cumul = cumul_all[:, heads + h : heads + h + 1]
                turned = turned_all[heads + h : heads + h + 1, :]
                last = turned[:, SPAN - 1 :]
                fading = jnp.exp(jnp.where(row_at >= col_at, cumul - turned, 0.0))
                grown = jnp.exp(cumul)
                jobs.append(
                    dict(
                        h=h,
                        lower=jnp.where(row_at > col_at, beta * fading * key_dots, 0.0),
                        attend=half(jnp.where(row_at >= col_at, fading * query_dots, 0.0)),
                        sides=half(jnp.concatenate([beta * grown * key, beta * value], 1)),
                        query=grown * query,
                        key_end=half(jnp.exp(last - cumul) * key),
                        fade=jnp.exp(last),
                    )
                )
        inverses = unit_inverses([job["lower"] for job in jobs], row_at, col_at)
        for job, inverse in zip(jobs, inverses):
            job["both"] = mm(inverse, job["sides"])
        return jobs

    blocks = tokens // SPAN
    prepared = {n: chunk(n) for n in range(1, blocks)}

    @pl.when(place > 0)
    def _():
        for copy in rims:
            copy.wait_recv()
        room[:EDGE, : 2 * key_cols] = rim_qk[...].astype(jnp.float32)
        room[:EDGE, 2 * key_cols :] = rim_value[...].astype(jnp.float32)

    @pl.when(place == 0)
    def _():
        room[:EDGE, :] = history[...].astype(jnp.float32)

    prepared[0] = chunk(0)
    none = jnp.zeros((SPAN, DV), jnp.float32)
    state = [None] * heads
    for n in range(blocks):
        rows = slice(n * SPAN, (n + 1) * SPAN)
        for job in prepared[n]:
            h, both = job["h"], job["both"]
            weights, updates = both[:, :KEY_HEAD_SIZE], both[:, KEY_HEAD_SIZE:]
            if n == 0:
                written = jnp.concatenate([-weights, updates], 1)
                seen = jnp.concatenate([job["query"], none], 1)
                carried = jnp.concatenate([job["fade"] * eye, none], 1)
            else:
                through = mm(jnp.concatenate([weights, job["query"]], 0), state[h])
                written = jnp.concatenate([none, updates], 1) - through[:SPAN]
                seen = through[SPAN:]
                carried = job["fade"] * state[h]
            readout = seen + mm(job["attend"], written)
            state[h] = carried + mm(job["key_end"], written, ((0,), (0,)))
            slope_ref[h, rows, :] = half(readout[:, :KEY_HEAD_SIZE])
            base_ref[h, rows, :] = readout[:, KEY_HEAD_SIZE:]
    for h in range(heads):
        maps_ref[h] = state[h]

    for h in range(heads):
        carry_map = half(maps_ref[h, :, :KEY_HEAD_SIZE])
        carry_add = half(maps_ref[h, :, KEY_HEAD_SIZE:].T)
        for c in range(cut):
            parts[h * cut + c, :KEY_HEAD_SIZE, :] = carry_map
            parts[h * cut + c, KEY_HEAD_SIZE:, :] = carry_add[c * tall : (c + 1) * tall]
    def part_copy(off):
        return pltpu.make_async_remote_copy(
            src_ref=parts.at[mate(off)],
            dst_ref=gathered.at[unit],
            send_sem=part_send.at[off],
            recv_sem=part_recv.at[off],
            device_id={"seq": first + mate(off)},
            device_id_type=mesh_id,
        )

    moving = [part_copy(off) for off in range(1, row)]
    for copy in moving:
        copy.start()
    gathered[unit] = parts[unit]
    for h in range(heads):
        turned = start_ref[h].T
        for c in range(cut):

            @pl.when(unit == h * cut + c)
            def _():
                entry[...] = turned[c * tall : (c + 1) * tall]

    for copy in fetches:
        copy.wait()
    gate_all = half(mm(hidden[...], w_gate[...])).astype(jnp.float32)
    for copy in moving:
        copy.wait()

    hop = pltpu.make_async_remote_copy(
        src_ref=hop_out,
        dst_ref=hop_in,
        send_sem=hop_send,
        recv_sem=hop_recv,
        device_id={"seq": lax.rem(place + row, count)},
        device_id_type=mesh_id,
    )

    def onward(values, n):
        top = half(values)
        rest = half(values - top.astype(jnp.float32))
        both = mm(
            jnp.concatenate([top, rest], 0), gathered[n, :KEY_HEAD_SIZE, :], ((1,), (1,))
        )
        return both[: values.shape[0]] + both[values.shape[0] :]

    def added(n):
        return gathered[n, KEY_HEAD_SIZE:, :].astype(jnp.float32)

    @pl.when(line > 0)
    def _():
        blank = jnp.zeros((KEY_HEAD_SIZE, KEY_HEAD_SIZE), jnp.float32)
        sweep = jnp.concatenate([eye, jnp.zeros((tall, KEY_HEAD_SIZE), jnp.float32)], 0)
        for n in range(row):
            sweep = onward(sweep, n) + jnp.concatenate([blank, added(n)], 0)
        whole = sweep[:KEY_HEAD_SIZE]
        top = half(whole)
        rest = half(whole - top.astype(jnp.float32))
        sides = jnp.concatenate([top, rest], 1)
        hop.wait_recv()
        came = hop_in[...]
        entry[...] = came
        came_top = half(came)
        came_rest = half(came - came_top.astype(jnp.float32))
        both = mm(jnp.concatenate([came_top, came_rest], 0), sides)
        hop_out[...] = (
            both[:tall, :KEY_HEAD_SIZE]
            + both[:tall, KEY_HEAD_SIZE:]
            + both[tall:, :KEY_HEAD_SIZE]
            + sweep[KEY_HEAD_SIZE:]
        )

        @pl.when(line < lines - 1)
        def _():
            hop.start()

    state = entry[...]
    before[0] = half(state)
    for n in range(row - 1):
        state = onward(state, n) + added(n)
        before[n + 1] = half(state)

    @pl.when(line == 0)
    def _():
        hop_out[...] = onward(state, row - 1) + added(row - 1)

        @pl.when(line < lines - 1)
        def _():
            hop.start()

    returning = [
        pltpu.make_async_remote_copy(
            src_ref=before.at[mate(off)],
            dst_ref=states.at[unit],
            send_sem=back_send.at[off],
            recv_sem=back_recv.at[off],
            device_id={"seq": first + mate(off)},
            device_id_type=mesh_id,
        )
        for off in range(1, row)
    ]
    for copy in returning:
        copy.start()
    states[unit] = before[unit]
    for copy in returning:
        copy.wait()

    pieces = []
    for h in range(heads):
        turned = jnp.concatenate([states[h * cut + c] for c in range(cut)], 0)
        gate = gate_all[:, h * DV : (h + 1) * DV]
        output = base_ref[h] + mm(slope_ref[h], turned, ((1,), (1,)))
        scale = lax.rsqrt(jnp.mean(output * output, axis=-1, keepdims=True) + 1e-06)
        pieces.append(half(output * scale * gain_ref[...] * silu(gate)))
    normed = jnp.concatenate(pieces, 1)
    wide = mixed_ref.shape[1]

    def term(where):
        columns = pl.ds(pl.multiple_of(where * wide, wide), wide)
        return mm(normed, w_ref[:, columns])

    chips = groups // 2
    core = lax.rem(group, 2)
    chip = group // 2

    def other(off):
        return 2 * lax.rem(chip + off, chips)

    def term_copy(slot, where):
        return pltpu.make_async_remote_copy(
            src_ref=terms.at[slot],
            dst_ref=landed.at[slot],
            send_sem=term_send.at[slot],
            recv_sem=term_recv.at[slot],
            device_id={"head": where},
            device_id_type=mesh_id,
        )

    order = [*range(1, chips), 0]
    near = {}
    for off in order:
        terms[off] = half(term(other(off) + 1 - core))
        near[off] = term_copy(off, 2 * chip + 1 - core)
        near[off].start()
    mine = {off: term(other(off) + core) for off in order}
    far = []
    for off in order[:-1]:
        near[off].wait()
        terms[chips + off] = half(mine[off] + landed[off].astype(jnp.float32))
        copy = term_copy(chips + off, other(off) + core)
        copy.start()
        far.append((chips + off, copy))
    for h in range(heads):
        turned = jnp.concatenate([states[h * cut + c] for c in range(cut)], 0)
        check_ref[h] = (
            mm(maps_ref[h, :, :KEY_HEAD_SIZE], turned, ((1,), (1,)))
            + maps_ref[h, :, KEY_HEAD_SIZE:]
        )
    near[0].wait()
    total = mine[0] + landed[0].astype(jnp.float32)
    for slot, copy in far:
        copy.wait()
        total = total + landed[slot].astype(jnp.float32)
    mixed_ref[...] = half(total)

    @pl.when(line < lines - 1)
    def _():
        hop.wait_send()

    @pl.when(place < count - 1)
    def _():
        for copy in rims:
            copy.wait_send()


def layer(
    pre_qk, pre_value, taps_qk, taps_value, history, gates, rows, state_in, gain,
    hidden, w_gate, w_out,
):
    tokens, model_width = hidden.shape
    heads = state_in.shape[0]
    count, groups = lax.axis_size("seq"), lax.axis_size("head")
    unit_count = min(2 * heads, count)
    tall = DV * heads // unit_count
    wide = model_width // groups
    room_wide = pre_qk.shape[1] + pre_value.shape[1]
    dma = pltpu.SemaphoreType.DMA
    bf16, f32 = jnp.bfloat16, jnp.float32
    return pl.pallas_call(
        functools.partial(layer_kernel, count=count, groups=groups),
        out_shape=[
            jax.ShapeDtypeStruct((tokens, wide), bf16),
            jax.ShapeDtypeStruct((heads, KEY_HEAD_SIZE, DV), f32),
        ],
        in_specs=[pl.BlockSpec(memory_space=pltpu.VMEM)] * 9
        + [pl.BlockSpec(memory_space=pl.ANY)] * 3,
        out_specs=[pl.BlockSpec(memory_space=pltpu.VMEM)] * 2,
        scratch_shapes=[
            pltpu.VMEM((EDGE + tokens, room_wide), f32),
            pltpu.VMEM((EDGE, pre_qk.shape[1]), bf16),
            pltpu.VMEM((EDGE, pre_value.shape[1]), bf16),
            pltpu.VMEM((heads, KEY_HEAD_SIZE, KEY_HEAD_SIZE + DV), f32),
            pltpu.VMEM((heads, tokens, DV), f32),
            pltpu.VMEM((heads, tokens, KEY_HEAD_SIZE), bf16),
            pltpu.VMEM(hidden.shape, bf16),
            pltpu.VMEM(w_gate.shape, bf16),
            pltpu.VMEM(w_out.shape, bf16),
            pltpu.VMEM((unit_count, KEY_HEAD_SIZE + tall, KEY_HEAD_SIZE), bf16),
            pltpu.VMEM((unit_count, KEY_HEAD_SIZE + tall, KEY_HEAD_SIZE), bf16),
            pltpu.VMEM((unit_count, tall, KEY_HEAD_SIZE), bf16),
            pltpu.VMEM((unit_count, tall, KEY_HEAD_SIZE), bf16),
            pltpu.VMEM((tall, KEY_HEAD_SIZE), f32),
            pltpu.VMEM((tall, KEY_HEAD_SIZE), f32),
            pltpu.VMEM((tall, KEY_HEAD_SIZE), f32),
            pltpu.VMEM((groups, tokens, wide), bf16),
            pltpu.VMEM((groups, tokens, wide), bf16),
            dma((3,)),
            dma((2,)),
            dma((2,)),
            dma((unit_count,)),
            dma((unit_count,)),
            dma((unit_count,)),
            dma((unit_count,)),
            dma(()),
            dma(()),
            dma((groups,)),
            dma((groups,)),
        ],
        compiler_params=pltpu.CompilerParams(
            collective_id=0, has_side_effects=True, vmem_limit_bytes=63 * 2**20
        ),
    )(
        pre_qk, pre_value, taps_qk, taps_value, history, gates, rows, state_in, gain,
        hidden, w_gate, w_out,
    )


def local(
    hidden_in,
    w_qk,
    w_value,
    w_outgate,
    w_ba,
    conv_qk,
    conv_value,
    hist_qk,
    hist_value,
    a_log,
    dt_bias,
    beta_bias,
    state_in,
    norm_gain,
    w_out,
):
    num_rows, model_width = hidden_in.shape
    key_cols = w_qk.shape[2]
    heads = a_log.shape[0]
    taps = conv_value.shape[0]
    qk_flat = w_qk.reshape(model_width, 2 * key_cols)
    pre_qk = stored(jnp.dot(hidden_in, qk_flat, preferred_element_type=jnp.float32))
    pre_value = stored(jnp.dot(hidden_in, w_value, preferred_element_type=jnp.float32))
    w_gates = jnp.pad(w_ba.reshape(model_width, 2 * heads), ((0, 0), (0, LANES - 2 * heads)))
    gates = stored(jnp.dot(hidden_in, w_gates, preferred_element_type=jnp.float32))
    history = jnp.concatenate([hist_qk.reshape(taps - 1, 2 * key_cols), hist_value], 1)
    history = jnp.pad(history, ((EDGE - (taps - 1), 0), (0, 0)))
    unused = jnp.zeros((LANES - 2 * heads,), jnp.float32)
    rows = jnp.stack(
        [
            jnp.concatenate([beta_bias, dt_bias, unused]),
            jnp.concatenate([a_log, a_log, unused]),
        ]
    )
    mixed, checkpoint = layer(
        pre_qk, pre_value, conv_qk.reshape(taps, 2 * key_cols), conv_value, history, gates, rows,
        state_in, norm_gain.reshape(1, -1), hidden_in, w_outgate, w_out,
    )
    return (mixed, checkpoint[None])


def solution(mesh):
    return jax.shard_map(
        local,
        mesh=mesh,
        in_specs=(
            P("seq", None),
            P(None, None, "head"),
            P(None, "head"),
            P(None, "head"),
            P(None, None, "head"),
            P(None, None, "head"),
            P(None, "head"),
            P(None, None, "head"),
            P(None, "head"),
            P("head"),
            P("head"),
            P("head"),
            P("head", None, None),
            P(),
            P("head", None),
        ),
        out_specs=(P("seq", "head"), P("seq", "head", None, None)),
        check_vma=False,
    )
```
